32 devices in a mesh: row: 4 (over x, core), col: 8 (over z, y).
Axes of the slice: x: 2, y: 2, z: 4, core: 2. Of those that a mesh axis runs over, the one named last changes fastest.
Arguments:
- optical_field: float32 [2, 512, 4096], P(None, 'row', 'col'), may hold values from -6 to 6
- index_panels: bfloat16 [5, 512, 4096], P(None, ('row', 'col')), may hold values from -4 to 4
Outputs:
- propagated: float32 [2, 512, 4096], P(None, 'row', 'col')
The draws below stay inside these ranges and needn't reach their ends.
All inputs are finite; a program needn't handle non-finite values.
Results may differ from the reference program's by a relative error of at most 0.0003.
Values may be sent and summed in bfloat16 or wider, within the bound.
A program may use at most 64 MiB of HBM per device.

```python
import jax
import jax.numpy as jnp

STEPS = 2
PLANES = 5
NY = 512
NX = 4096


def levels(key, shape, pieces, least, top_value):
    def one(axis_at, parts):
        steps = jax.random.uniform(jax.random.fold_in(jax.random.fold_in(key, 6), axis_at), (parts,), jnp.float32, least / len(pieces), top_value / len(pieces))
        return jnp.repeat(jnp.exp(steps), shape[axis_at] // parts).reshape((-1,) + (1,) * (len(shape) - axis_at - 1))

    factor_of = one(*pieces[0])
    for cut in pieces[1:]:
        factor_of = factor_of * one(*cut)
    return factor_of


def gaussian(rng, extent, spread, bound, cuts=(), held_as=jnp.bfloat16):
    result = jax.random.normal(rng, extent, jnp.float32) * spread
    if len(cuts) > 0:
        result = levels(rng, extent, cuts, -0.22, 0.18) * result
    return jnp.clip(result, min=-bound, max=bound).astype(held_as)


def setup_inputs(seed: int = 0) -> dict:
    splits = jax.random.split(jax.random.key(seed), 3)
    optical_field = gaussian(splits[0], (2, NY, NX), 1.0, 6.0, ((1, 4), (2, 8)), jnp.float32)
    index_panels = gaussian(splits[1], (PLANES, NY, NX), 1.0, 4.0, ((1, 32),))
    return {"optical_field": optical_field, "index_panels": index_panels}


diffraction = 0.15
phase_gain = 0.25


def laplace(values):
    along_y = 16.0 * (jnp.roll(values, 1, 1) + jnp.roll(values, -1, 1)) - (jnp.roll(values, 2, 1) + jnp.roll(values, -2, 1))
    along_x = 16.0 * (jnp.roll(values, 1, 2) + jnp.roll(values, -1, 2)) - (jnp.roll(values, 2, 2) + jnp.roll(values, -2, 2))
    return (along_y + along_x - 60.0 * values) / 12.0


def slope(values, plane):
    total = diffraction * laplace(values) + phase_gain * plane.astype(jnp.float32) * values
    return jnp.stack([-total[1], total[0]])


def reference(optical_field, index_panels):
    field = optical_field
    for step_index in range(STEPS):
        first = 2 * step_index
        first_slope = slope(field, index_panels[first])
        second_slope = slope(field + 0.5 * first_slope, index_panels[first + 1])
        third_slope = slope(field + 0.5 * second_slope, index_panels[first + 1])
        fourth_slope = slope(field + third_slope, index_panels[first + 2])
        field = field + (first_slope + 2.0 * second_slope + 2.0 * third_slope + fourth_slope) / 6.0
    return field
```

```python
import functools

import jax
import jax.numpy as jnp
from jax import lax
from jax.experimental import pallas as pl
from jax.experimental.pallas import tpu as pltpu
from jax.sharding import PartitionSpec as P

STEPS = 2
MESH = pl.DeviceIdType.MESH
HALO = 16
PAD = 8
LANES = 128

diffraction = 0.15
phase_gain = 0.25
near = diffraction * 16.0 / 12.0
far = diffraction / 12.0
mid = diffraction * 60.0 / 12.0


def kernel(nr, nc, field, panels_in, out, panels, pack, planes, e, s1, s2, s3,
           strips, side, corners, load_sem, send_sem, plane_recv, fwd_send, fwd_recv,
           halo_send, halo_recv):
    n_planes, part, width = panels.shape
    _, rows, cols = out.shape
    wide = cols + LANES
    sub = HALO // part
    top = PAD + HALO
    last = n_planes - 1
    r, c = lax.axis_index("row"), lax.axis_index("col")
    up, down = lax.rem(r + nr - 1, nr), lax.rem(r + 1, nr)
    left, right = lax.rem(c + nc - 1, nc), lax.rem(c + 1, nc)

    load_field = pltpu.make_async_copy(field, e.at[:, pl.ds(top, rows), pl.ds(0, cols)], load_sem.at[0])
    load_field.start()
    load_panels = pltpu.make_async_copy(panels_in, panels, load_sem.at[1])
    load_panels.start()

    barrier = pltpu.get_barrier_semaphore()
    peers = [(r, lax.rem(c + k, nc)) for k in range(1, nc)]
    peers += [(y, x) for y in (up, down) for x in (left, c, right)]
    for peer in peers:
        pl.semaphore_signal(barrier, inc=1, device_id=peer, device_id_type=MESH)

    lane = lax.broadcasted_iota(jnp.int32, (part, LANES), 1)
    load_panels.wait()

    def pack_plane(p):
        for d in range(nc):
            pack[p, d, :, 0:cols] = panels[p, :, d * cols:(d + 1) * cols]
            if p < last:
                after = (d + 1) * cols % width
                before = (d * cols - LANES) % width
                pack[p, d, :, cols:wide] = jnp.where(
                    lane < LANES // 2,
                    panels[p, :, after:after + LANES].astype(jnp.float32),
                    panels[p, :, before:before + LANES].astype(jnp.float32),
                ).astype(pack.dtype)

    def plane_copy(p, k):
        to = lax.rem(c + k, nc)
        span = wide if p < last else cols
        return pltpu.make_async_remote_copy(
            src_ref=pack.at[p, to, :, pl.ds(0, span)],
            dst_ref=planes.at[p, sub + c, :, pl.ds(0, span)],
            send_sem=send_sem.at[p, k],
            recv_sem=plane_recv.at[p, k],
            device_id=(r, to),
            device_id_type=MESH,
        )

    def send_plane(p):
        for k in range(1, nc):
            plane_copy(p, k).start()
        planes[p, sub + c] = pack[p, c]

    pack_plane(0)
    load_field.wait()
    for i in range(2):
        strips[0, i] = e[i, top:top + rows, 0:LANES].T[0:HALO]
        strips[1, i] = e[i, top:top + rows, cols - LANES:cols].T[LANES - HALO:LANES]

    def remote(src, dst, at, to):
        return pltpu.make_async_remote_copy(
            src_ref=src, dst_ref=dst, send_sem=halo_send.at[at], recv_sem=halo_recv.at[at],
            device_id=to, device_id_type=MESH,
        )

    low, high = pl.ds(0, HALO), pl.ds(rows - HALO, HALO)
    first_tile, last_tile = pl.ds(0, LANES), pl.ds(cols - LANES, LANES)
    halos = [
        remote(field.at[:, high, :], e.at[:, pl.ds(PAD, HALO), pl.ds(0, cols)], 0, (down, c)),
        remote(field.at[:, low, :], e.at[:, pl.ds(top + rows, HALO), pl.ds(0, cols)], 1, (up, c)),
        remote(strips.at[0], side.at[:, pl.ds(0, HALO), :], 2, (r, left)),
        remote(strips.at[1], side.at[:, pl.ds(LANES - HALO, HALO), :], 3, (r, right)),
        remote(field.at[:, high, first_tile], corners.at[0], 4, (down, left)),
        remote(field.at[:, high, last_tile], corners.at[1], 5, (down, right)),
        remote(field.at[:, low, first_tile], corners.at[2], 6, (up, left)),
        remote(field.at[:, low, last_tile], corners.at[3], 7, (up, right)),
    ]

    pl.semaphore_wait(barrier, len(peers))
    for copy in halos:
        copy.start()
    send_plane(0)
    for p in range(1, n_planes):
        pack_plane(p)
        send_plane(p)

    for copy in halos:
        copy.wait()
    tile_lane = lax.broadcasted_iota(jnp.int32, (HALO, LANES), 1)
    for i in range(2):
        e[i, top:top + rows, cols:wide] = side[i].T
        e[i, PAD:top, cols:wide] = jnp.where(tile_lane < LANES // 2, corners[0, i], corners[1, i])
        e[i, top + rows:top + rows + HALO, cols:wide] = jnp.where(
            tile_lane < LANES // 2, corners[2, i], corners[3, i])

    def forwards(p):
        blocks = rows // part
        make = lambda src, dst, at, to: pltpu.make_async_remote_copy(
            src_ref=planes.at[p, pl.ds(src, sub)], dst_ref=planes.at[p, pl.ds(dst, sub)],
            send_sem=fwd_send.at[p, at], recv_sem=fwd_recv.at[p, at],
            device_id=(to, c), device_id_type=MESH,
        )
        return [make(blocks, 0, 0, down), make(sub, sub + blocks, 1, up)]

    def take_plane(p):
        for k in range(1, nc):
            plane_copy(p, k).wait_recv()
        if p < last:
            copies = forwards(p)
            for copy in copies:
                copy.start()
            for copy in copies:
                copy.wait()

    def evaluate(src, p, begin, end, finish):
        def block(b, carry):
            row = pl.multiple_of(b * HALO, HALO)
            if sub == 1:
                plane = planes[p, b].astype(jnp.float32)
            else:
                plane = jnp.concatenate(
                    [planes[p, b * sub + i].astype(jnp.float32) for i in range(sub)], axis=0)
            factor = phase_gain * plane - mid
            totals = []
            for i in range(2):
                window = src[i, pl.ds(row, HALO + 2 * PAD), :]
                tall = HALO + 2 * PAD
                centre = window[PAD:PAD + HALO]
                shift_y = lambda n: pltpu.roll(window, n % tall, 0)[PAD:PAD + HALO]
                shift_x = lambda n: pltpu.roll(centre, n % wide, 1)
                one = (shift_y(1) + shift_y(-1)) + (shift_x(1) + shift_x(-1))
                two = (shift_y(2) + shift_y(-2)) + (shift_x(2) + shift_x(-2))
                totals.append(near * one - far * two + factor * centre)
            finish(pl.ds(pl.multiple_of(row + PAD, PAD), HALO), b, (-totals[1], totals[0]))
            return carry

        lax.fori_loop(begin, end, block, 0)

    def stage(dst, weight):
        def finish(at, b, k):
            for i in range(2):
                dst[i, at, :] = e[i, at, :] + weight * k[i]
        return finish

    def close(at, b, k):
        for i in range(2):
            e[i, at, :] = (s1[i, at, :] + 2.0 * s2[i, at, :] + s3[i, at, :] - e[i, at, :]) * (1.0 / 3.0) + k[i] * (1.0 / 6.0)

    def close_out(at, b, k):
        here = pl.ds(pl.multiple_of((b - 1) * HALO, HALO), HALO)
        for i in range(2):
            value = (s1[i, at, :] + 2.0 * s2[i, at, :] + s3[i, at, :] - e[i, at, :]) * (1.0 / 3.0) + k[i] * (1.0 / 6.0)
            out[i, here, :] = value[:, 0:cols]

    full = rows // HALO + 2
    take_plane(0)
    for step in range(STEPS):
        p = 2 * step
        evaluate(e, p, 0, full, stage(s1, 0.5))
        take_plane(p + 1)
        evaluate(s1, p + 1, 0, full, stage(s2, 0.5))
        evaluate(s2, p + 1, 0, full, stage(s3, 1.0))
        take_plane(p + 2)
        if step < STEPS - 1:
            evaluate(s3, p + 2, 0, full, close)
        else:
            evaluate(s3, p + 2, 1, full - 1, close_out)

    for p in range(n_planes):
        for k in range(1, nc):
            plane_copy(p, k).wait_send()


def solution(mesh):
    nr, nc = mesh.shape["row"], mesh.shape["col"]

    def local(optical_field, index_panels):
        _, rows, cols = optical_field.shape
        n_planes, part, width = index_panels.shape
        wide = cols + LANES
        tall = rows + 2 * HALO + 2 * PAD
        grid = pltpu.VMEM((2, tall, wide), jnp.float32)
        return pl.pallas_call(
            functools.partial(kernel, nr, nc),
            out_shape=jax.ShapeDtypeStruct(optical_field.shape, jnp.float32),
            in_specs=[pl.BlockSpec(memory_space=pl.ANY)] * 2,
            out_specs=pl.BlockSpec(memory_space=pltpu.VMEM),
            scratch_shapes=[
                pltpu.VMEM((n_planes, part, width), jnp.bfloat16),
                pltpu.VMEM((n_planes, nc, part, wide), jnp.bfloat16),
                pltpu.VMEM((n_planes, (rows + 2 * HALO) // part, part, wide), jnp.bfloat16),
                grid, grid, grid, grid,
                pltpu.VMEM((2, 2, HALO, rows), jnp.float32),
                pltpu.VMEM((2, LANES, rows), jnp.float32),
                pltpu.VMEM((4, 2, HALO, LANES), jnp.float32),
                pltpu.SemaphoreType.DMA((2,)),
                pltpu.SemaphoreType.DMA((n_planes, nc)),
                pltpu.SemaphoreType.DMA((n_planes, nc)),
                pltpu.SemaphoreType.DMA((n_planes, 2)),
                pltpu.SemaphoreType.DMA((n_planes, 2)),
                pltpu.SemaphoreType.DMA((8,)),
                pltpu.SemaphoreType.DMA((8,)),
            ],
            compiler_params=pltpu.CompilerParams(
                collective_id=0, has_side_effects=True, vmem_limit_bytes=48 * 1024 * 1024),
        )(optical_field, index_panels)

    return jax.shard_map(
        local, mesh=mesh,
        in_specs=(P(None, "row", "col"), P(None, ("row", "col"), None)),
        out_specs=P(None, "row", "col"), check_vma=False,
    )
```

```python
import functools

import jax
import jax.numpy as jnp
from jax import lax
from jax.experimental import pallas as pl
from jax.experimental.pallas import tpu as pltpu
from jax.sharding import PartitionSpec as P

STEPS = 2
MESH = pl.DeviceIdType.MESH
HALO = 16
PAD = 8
LANES = 128

diffraction = 0.15
phase_gain = 0.25
near = diffraction * 16.0 / 12.0
far = diffraction / 12.0
mid = diffraction * 60.0 / 12.0


def kernel(nr, nc, ahead, field, panels_in, out, panels, pack, gathered, planes, edges, e, s1, s2, s3,
           strips, side, corners, load_sem, send_sem, plane_recv, edge_send, edge_recv, fwd_send, fwd_recv,
           halo_send, halo_recv):
    n_planes, part, width = panels.shape
    _, rows, cols = out.shape
    wide = cols + LANES
    sub = HALO // part
    blocks = rows // part
    top = PAD + HALO
    last = n_planes - 1
    pair = 2 * HALO
    r, c = lax.axis_index("row"), lax.axis_index("col")
    up, down = lax.rem(r + nr - 1, nr), lax.rem(r + 1, nr)
    left, right = lax.rem(c + nc - 1, nc), lax.rem(c + 1, nc)

    barrier = pltpu.get_barrier_semaphore()
    peers = [(r, lax.rem(c + k, nc)) for k in range(1, nc)]
    peers += [(y, x) for y in (up, down) for x in (left, c, right)]
    for peer in peers:
        pl.semaphore_signal(barrier, inc=1, device_id=peer, device_id_type=MESH)

    load_field = pltpu.make_async_copy(field, e.at[:, pl.ds(top, rows), pl.ds(0, cols)], load_sem.at[0])
    load_field.start()
    load_panels = pltpu.make_async_copy(panels_in, panels, load_sem.at[1])
    load_panels.start()
    own_columns = pl.ds(pl.multiple_of(c * cols, LANES), cols)
    own_planes = pltpu.make_async_copy(panels_in.at[:, :, own_columns], planes.at[:, sub + c], load_sem.at[2])
    own_planes.start()

    lane = lax.broadcasted_iota(jnp.int32, (part, LANES), 1)
    load_panels.wait()
    for d in range(nc):
        after = (d + 1) * cols % width
        before = (d * cols - LANES) % width
        tile = jnp.zeros((part, LANES), jnp.float32)
        for p in range(last):
            at = pair * p
            tile = jnp.where((lane >= at) & (lane < at + HALO), pltpu.roll(
                panels[p, :, after:after + LANES].astype(jnp.float32), at, 1), tile)
            at += HALO
            tile = jnp.where((lane >= at) & (lane < at + HALO), pltpu.roll(
                panels[p, :, before:before + LANES].astype(jnp.float32), (at + HALO) % LANES, 1), tile)
        pack[d] = tile.astype(pack.dtype)

    load_field.wait()
    for i in range(2):
        strips[0, i] = e[i, top:top + rows, 0:LANES].T[0:HALO]
        strips[1, i] = e[i, top:top + rows, cols - LANES:cols].T[LANES - HALO:LANES]

    def plane_copy(p, k):
        to = lax.rem(c + k, nc)
        return pltpu.make_async_remote_copy(
            src_ref=panels_in.at[p, :, pl.ds(pl.multiple_of(to * cols, LANES), cols)],
            dst_ref=planes.at[p, sub + c],
            send_sem=send_sem.at[p, k], recv_sem=plane_recv.at[p, k],
            device_id=(r, to), device_id_type=MESH,
        )

    def send_plane(p):
        for k in range(1, nc):
            plane_copy(p, k).start()

    def edge_copy(k):
        to = lax.rem(c + k, nc)
        return pltpu.make_async_remote_copy(
            src_ref=pack.at[to], dst_ref=gathered.at[sub + c],
            send_sem=edge_send.at[k], recv_sem=edge_recv.at[k],
            device_id=(r, to), device_id_type=MESH,
        )

    def remote(src, dst, at, to):
        return pltpu.make_async_remote_copy(
            src_ref=src, dst_ref=dst, send_sem=halo_send.at[at], recv_sem=halo_recv.at[at],
            device_id=to, device_id_type=MESH,
        )

    low, high = pl.ds(0, HALO), pl.ds(rows - HALO, HALO)
    first_tile, last_tile = pl.ds(0, LANES), pl.ds(cols - LANES, LANES)
    halos = [
        remote(field.at[:, high, :], e.at[:, pl.ds(PAD, HALO), pl.ds(0, cols)], 0, (down, c)),
        remote(field.at[:, low, :], e.at[:, pl.ds(top + rows, HALO), pl.ds(0, cols)], 1, (up, c)),
        remote(strips.at[0], side.at[:, pl.ds(0, HALO), :], 2, (r, left)),
        remote(strips.at[1], side.at[:, pl.ds(LANES - HALO, HALO), :], 3, (r, right)),
        remote(field.at[:, high, first_tile], corners.at[0], 4, (down, left)),
        remote(field.at[:, high, last_tile], corners.at[1], 5, (down, right)),
        remote(field.at[:, low, first_tile], corners.at[2], 6, (up, left)),
        remote(field.at[:, low, last_tile], corners.at[3], 7, (up, right)),
    ]

    pl.semaphore_wait(barrier, len(peers))
    for k in range(1, nc):
        edge_copy(k).start()
    for copy in halos:
        copy.start()
    for p in range(ahead):
        send_plane(p)
    gathered[sub + c] = pack[c]

    def forwards(ref, at):
        make = lambda src, dst, which, to: pltpu.make_async_remote_copy(
            src_ref=ref.at[pl.ds(src, sub)], dst_ref=ref.at[pl.ds(dst, sub)],
            send_sem=fwd_send.at[at, which], recv_sem=fwd_recv.at[at, which],
            device_id=(to, c), device_id_type=MESH,
        )
        return [make(blocks, 0, 0, down), make(sub, sub + blocks, 1, up)]

    for k in range(1, nc):
        edge_copy(k).wait_recv()
    edge_forwards = forwards(gathered, last)
    for copy in edge_forwards:
        copy.start()

    for copy in halos:
        copy.wait()
    tile_lane = lax.broadcasted_iota(jnp.int32, (HALO, LANES), 1)
    for i in range(2):
        e[i, top:top + rows, cols:wide] = side[i].T
        e[i, PAD:top, cols:wide] = jnp.where(tile_lane < LANES // 2, corners[0, i], corners[1, i])
        e[i, top + rows:top + rows + HALO, cols:wide] = jnp.where(
            tile_lane < LANES // 2, corners[2, i], corners[3, i])

    for copy in edge_forwards:
        copy.wait()
    for b in range(blocks + 2 * sub):
        tile = gathered[b].astype(jnp.float32)
        for p in range(last):
            edges[p, b] = jnp.where(
                lane < LANES // 2,
                pltpu.roll(tile, (LANES - pair * p) % LANES, 1),
                pltpu.roll(tile, (LANES - pair * (p + 1)) % LANES, 1),
            ).astype(edges.dtype)
    own_planes.wait()

    def take_plane(p):
        for k in range(1, nc):
            plane_copy(p, k).wait_recv()
        copies = forwards(planes.at[p], p) if p < last else []
        for copy in copies:
            copy.start()
        if p + ahead < n_planes:
            send_plane(p + ahead)
        for copy in copies:
            copy.wait()

    def evaluate(src, p, begin, end, finish):
        def block(b, carry):
            row = pl.multiple_of(b * HALO, HALO)
            pieces = []
            for i in range(sub):
                piece = planes[p, b * sub + i].astype(jnp.float32)
                edge = edges[min(p, last - 1), b * sub + i].astype(jnp.float32)
                pieces.append(jnp.concatenate([piece, edge], axis=1))
            plane = pieces[0] if sub == 1 else jnp.concatenate(pieces, axis=0)
            factor = phase_gain * plane - mid
            totals = []
            for i in range(2):
                window = src[i, pl.ds(row, HALO + 2 * PAD), :]
                tall = HALO + 2 * PAD
                centre = window[PAD:PAD + HALO]
                shift_y = lambda n: pltpu.roll(window, n % tall, 0)[PAD:PAD + HALO]
                shift_x = lambda n: pltpu.roll(centre, n % wide, 1)
                one = (shift_y(1) + shift_y(-1)) + (shift_x(1) + shift_x(-1))
                two = (shift_y(2) + shift_y(-2)) + (shift_x(2) + shift_x(-2))
                totals.append(near * one - far * two + factor * centre)
            finish(pl.ds(pl.multiple_of(row + PAD, PAD), HALO), b, (-totals[1], totals[0]))
            return carry

        lax.fori_loop(begin, end, block, 0, unroll=end - begin)

    def stage(dst, weight):
        def finish(at, b, k):
            for i in range(2):
                dst[i, at, :] = e[i, at, :] + weight * k[i]
        return finish

    def close(at, b, k):
        for i in range(2):
            e[i, at, :] = (s1[i, at, :] + 2.0 * s2[i, at, :] + s3[i, at, :] - e[i, at, :]) * (1.0 / 3.0) + k[i] * (1.0 / 6.0)

    def close_out(at, b, k):
        here = pl.ds(pl.multiple_of((b - 1) * HALO, HALO), HALO)
        for i in range(2):
            value = (s1[i, at, :] + 2.0 * s2[i, at, :] + s3[i, at, :] - e[i, at, :]) * (1.0 / 3.0) + k[i] * (1.0 / 6.0)
            out[i, here, :] = value[:, 0:cols]

    full = rows // HALO + 2
    take_plane(0)
    for step in range(STEPS):
        p = 2 * step
        evaluate(e, p, 0, full, stage(s1, 0.5))
        take_plane(p + 1)
        evaluate(s1, p + 1, 0, full, stage(s2, 0.5))
        evaluate(s2, p + 1, 0, full, stage(s3, 1.0))
        take_plane(p + 2)
        if step < STEPS - 1:
            evaluate(s3, p + 2, 0, full, close)
        else:
            evaluate(s3, p + 2, 1, full - 1, close_out)

    for k in range(1, nc):
        edge_copy(k).wait_send()
        for p in range(n_planes):
            plane_copy(p, k).wait_send()


def solution(mesh):
    nr, nc = mesh.shape["row"], mesh.shape["col"]

    def local(optical_field, index_panels):
        _, rows, cols = optical_field.shape
        n_planes, part, width = index_panels.shape
        wide = cols + LANES
        count = (rows + 2 * HALO) // part
        tall = rows + 2 * HALO + 2 * PAD
        grid = pltpu.VMEM((2, tall, wide), jnp.float32)
        return pl.pallas_call(
            functools.partial(kernel, nr, nc, 2),
            out_shape=jax.ShapeDtypeStruct(optical_field.shape, jnp.float32),
            in_specs=[pl.BlockSpec(memory_space=pltpu.HBM)] * 2,
            out_specs=pl.BlockSpec(memory_space=pltpu.VMEM),
            scratch_shapes=[
                pltpu.VMEM((n_planes, part, width), jnp.bfloat16),
                pltpu.VMEM((nc, part, LANES), jnp.bfloat16),
                pltpu.VMEM((count, part, LANES), jnp.bfloat16),
                pltpu.VMEM((n_planes, count, part, cols), jnp.bfloat16),
                pltpu.VMEM((n_planes - 1, count, part, LANES), jnp.bfloat16),
                grid, grid, grid, grid,
                pltpu.VMEM((2, 2, HALO, rows), jnp.float32),
                pltpu.VMEM((2, LANES, rows), jnp.float32),
                pltpu.VMEM((4, 2, HALO, LANES), jnp.float32),
                pltpu.SemaphoreType.DMA((3,)),
                pltpu.SemaphoreType.DMA((n_planes, nc)),
                pltpu.SemaphoreType.DMA((n_planes, nc)),
                pltpu.SemaphoreType.DMA((nc,)),
                pltpu.SemaphoreType.DMA((nc,)),
                pltpu.SemaphoreType.DMA((n_planes, 2)),
                pltpu.SemaphoreType.DMA((n_planes, 2)),
                pltpu.SemaphoreType.DMA((8,)),
                pltpu.SemaphoreType.DMA((8,)),
            ],
            compiler_params=pltpu.CompilerParams(
                collective_id=0, has_side_effects=True, vmem_limit_bytes=63 * 1024 * 1024),
        )(optical_field, index_panels)

    return jax.shard_map(
        local, mesh=mesh,
        in_specs=(P(None, "row", "col"), P(None, ("row", "col"), None)),
        out_specs=P(None, "row", "col"), check_vma=False,
    )
```

```python
import functools

import jax
import jax.numpy as jnp
from jax import lax
from jax.experimental import pallas as pl
from jax.experimental.pallas import tpu as pltpu
from jax.sharding import PartitionSpec as P

STEPS = 2
MESH = pl.DeviceIdType.MESH
HALO = 16
PAD = 8
LANES = 128

diffraction = 0.15
phase_gain = 0.25
near = diffraction * 16.0 / 12.0
far = diffraction / 12.0
mid = diffraction * 60.0 / 12.0


def kernel(nr, nc, ahead, field, panels_in, out, panels, pack, gathered, planes, edges, e, s1, s2, s3,
           strips, side, corners, load_sem, send_sem, plane_recv, edge_send, edge_recv, fwd_send, fwd_recv,
           halo_send, halo_recv):
    n_planes, part, width = panels.shape
    _, rows, cols = out.shape
    wide = cols + LANES
    sub = HALO // part
    blocks = rows // part
    top = PAD + HALO
    last = n_planes - 1
    pair = 2 * HALO
    r, c = lax.axis_index("row"), lax.axis_index("col")
    up, down = lax.rem(r + nr - 1, nr), lax.rem(r + 1, nr)
    left, right = lax.rem(c + nc - 1, nc), lax.rem(c + 1, nc)

    barrier = pltpu.get_barrier_semaphore()
    peers = [(r, lax.rem(c + k, nc)) for k in range(1, nc)]
    peers += [(y, x) for y in (up, down) for x in (left, c, right)]
    for peer in peers:
        pl.semaphore_signal(barrier, inc=1, device_id=peer, device_id_type=MESH)

    load_field = pltpu.make_async_copy(field, e.at[:, pl.ds(top, rows), pl.ds(0, cols)], load_sem.at[0])
    load_field.start()
    load_panels = pltpu.make_async_copy(panels_in, panels, load_sem.at[1])
    load_panels.start()
    own_columns = pl.ds(pl.multiple_of(c * cols, LANES), cols)
    own_planes = pltpu.make_async_copy(panels_in.at[:, :, own_columns], planes.at[:, sub + c], load_sem.at[2])
    own_planes.start()

    def plane_copy(p, k):
        to = lax.rem(c + k, nc)
        return pltpu.make_async_remote_copy(
            src_ref=panels_in.at[p, :, pl.ds(pl.multiple_of(to * cols, LANES), cols)],
            dst_ref=planes.at[p, sub + c],
            send_sem=send_sem.at[p, k], recv_sem=plane_recv.at[p, k],
            device_id=(r, to), device_id_type=MESH,
        )

    def send_plane(p):
        for k in range(1, nc):
            plane_copy(p, k).start()

    def edge_copy(k):
        to = lax.rem(c + k, nc)
        return pltpu.make_async_remote_copy(
            src_ref=pack.at[to], dst_ref=gathered.at[sub + c],
            send_sem=edge_send.at[k], recv_sem=edge_recv.at[k],
            device_id=(r, to), device_id_type=MESH,
        )

    def remote(src, dst, at, to):
        return pltpu.make_async_remote_copy(
            src_ref=src, dst_ref=dst, send_sem=halo_send.at[at], recv_sem=halo_recv.at[at],
            device_id=to, device_id_type=MESH,
        )

    low, high = pl.ds(0, HALO), pl.ds(rows - HALO, HALO)
    first_tile, last_tile = pl.ds(0, LANES), pl.ds(cols - LANES, LANES)
    halos = [
        remote(field.at[:, high, :], e.at[:, pl.ds(PAD, HALO), pl.ds(0, cols)], 0, (down, c)),
        remote(field.at[:, low, :], e.at[:, pl.ds(top + rows, HALO), pl.ds(0, cols)], 1, (up, c)),
        remote(strips.at[0], side.at[:, pl.ds(0, HALO), :], 2, (r, left)),
        remote(strips.at[1], side.at[:, pl.ds(LANES - HALO, HALO), :], 3, (r, right)),
        remote(field.at[:, high, first_tile], corners.at[0], 4, (down, left)),
        remote(field.at[:, high, last_tile], corners.at[1], 5, (down, right)),
        remote(field.at[:, low, first_tile], corners.at[2], 6, (up, left)),
        remote(field.at[:, low, last_tile], corners.at[3], 7, (up, right)),
    ]

    pl.semaphore_wait(barrier, len(peers))
    for copy in halos[:2] + halos[4:]:
        copy.start()
    send_plane(0)
    load_field.wait()
    for i in range(2):
        strips[0, i] = e[i, top:top + rows, 0:LANES].T[0:HALO]
        strips[1, i] = e[i, top:top + rows, cols - LANES:cols].T[LANES - HALO:LANES]

    for copy in halos[2:4]:
        copy.start()

    lane = lax.broadcasted_iota(jnp.int32, (part, LANES), 1)
    load_panels.wait()
    for d in range(nc):
        after = (d + 1) * cols % width
        before = (d * cols - LANES) % width
        tile = jnp.zeros((part, LANES), jnp.float32)
        for p in range(last):
            at = pair * p
            tile = jnp.where((lane >= at) & (lane < at + HALO), pltpu.roll(
                panels[p, :, after:after + LANES].astype(jnp.float32), at, 1), tile)
            at += HALO
            tile = jnp.where((lane >= at) & (lane < at + HALO), pltpu.roll(
                panels[p, :, before:before + LANES].astype(jnp.float32), (at + HALO) % LANES, 1), tile)
        pack[d] = tile.astype(pack.dtype)

    for k in range(1, nc):
        edge_copy(k).start()
    for p in range(1, ahead):
        send_plane(p)
    gathered[sub + c] = pack[c]

    def forwards(ref, at):
        make = lambda src, dst, which, to: pltpu.make_async_remote_copy(
            src_ref=ref.at[pl.ds(src, sub)], dst_ref=ref.at[pl.ds(dst, sub)],
            send_sem=fwd_send.at[at, which], recv_sem=fwd_recv.at[at, which],
            device_id=(to, c), device_id_type=MESH,
        )
        return [make(blocks, 0, 0, down), make(sub, sub + blocks, 1, up)]

    for k in range(1, nc):
        edge_copy(k).wait_recv()
    edge_forwards = forwards(gathered, last)
    for copy in edge_forwards:
        copy.start()

    for copy in halos:
        copy.wait()
    tile_lane = lax.broadcasted_iota(jnp.int32, (HALO, LANES), 1)
    for i in range(2):
        e[i, top:top + rows, cols:wide] = side[i].T
        e[i, PAD:top, cols:wide] = jnp.where(tile_lane < LANES // 2, corners[0, i], corners[1, i])
        e[i, top + rows:top + rows + HALO, cols:wide] = jnp.where(
            tile_lane < LANES // 2, corners[2, i], corners[3, i])

    for copy in edge_forwards:
        copy.wait()
    for b in range(blocks + 2 * sub):
        tile = gathered[b].astype(jnp.float32)
        for p in range(last):
            edges[p, b] = jnp.where(
                lane < LANES // 2,
                pltpu.roll(tile, (LANES - pair * p) % LANES, 1),
                pltpu.roll(tile, (LANES - pair * (p + 1)) % LANES, 1),
            ).astype(edges.dtype)
    own_planes.wait()

    def take_plane(p):
        for k in range(1, nc):
            plane_copy(p, k).wait_recv()
        copies = forwards(planes.at[p], p) if p < last else []
        for copy in copies:
            copy.start()
        if p + ahead < n_planes:
            send_plane(p + ahead)
        return copies

    def evaluate(src, p, begin, end, finish, stride=1):
        def block(n, carry):
            b = n * stride
            row = pl.multiple_of(b * HALO, HALO)
            pieces = []
            for i in range(sub):
                piece = planes[p, b * sub + i].astype(jnp.float32)
                edge = edges[min(p, last - 1), b * sub + i].astype(jnp.float32)
                pieces.append(jnp.concatenate([piece, edge], axis=1))
            plane = pieces[0] if sub == 1 else jnp.concatenate(pieces, axis=0)
            factor = phase_gain * plane - mid
            totals = []
            for i in range(2):
                window = src[i, pl.ds(row, HALO + 2 * PAD), :]
                tall = HALO + 2 * PAD
                centre = window[PAD:PAD + HALO]
                shift_y = lambda n: pltpu.roll(window, n % tall, 0)[PAD:PAD + HALO]
                shift_x = lambda n: pltpu.roll(centre, n % wide, 1)
                one = (shift_y(1) + shift_y(-1)) + (shift_x(1) + shift_x(-1))
                two = (shift_y(2) + shift_y(-2)) + (shift_x(2) + shift_x(-2))
                totals.append(near * one - far * two + factor * centre)
            finish(pl.ds(pl.multiple_of(row + PAD, PAD), HALO), b, (-totals[1], totals[0]))
            return carry

        lax.fori_loop(begin, end, block, 0, unroll=end - begin)

    def stage(dst, weight):
        def finish(at, b, k):
            for i in range(2):
                dst[i, at, :] = e[i, at, :] + weight * k[i]
        return finish

    def close(at, b, k):
        for i in range(2):
            e[i, at, :] = (s1[i, at, :] + 2.0 * s2[i, at, :] + s3[i, at, :] - e[i, at, :]) * (1.0 / 3.0) + k[i] * (1.0 / 6.0)

    def close_out(at, b, k):
        here = pl.ds(pl.multiple_of((b - 1) * HALO, HALO), HALO)
        for i in range(2):
            value = (s1[i, at, :] + 2.0 * s2[i, at, :] + s3[i, at, :] - e[i, at, :]) * (1.0 / 3.0) + k[i] * (1.0 / 6.0)
            out[i, here, :] = value[:, 0:cols]

    full = rows // HALO + 2

    def first_evaluate(src, p, finish):
        copies = take_plane(p)
        evaluate(src, p, 1, full - 1, finish)
        for copy in copies:
            copy.wait()
        evaluate(src, p, 0, 2, finish, full - 1)

    for step in range(STEPS):
        p = 2 * step
        if step == 0:
            first_evaluate(e, p, stage(s1, 0.5))
        else:
            evaluate(e, p, 0, full, stage(s1, 0.5))
        first_evaluate(s1, p + 1, stage(s2, 0.5))
        evaluate(s2, p + 1, 0, full, stage(s3, 1.0))
        if step < STEPS - 1:
            first_evaluate(s3, p + 2, close)
        else:
            take_plane(p + 2)
            evaluate(s3, p + 2, 1, full - 1, close_out)

    for k in range(1, nc):
        edge_copy(k).wait_send()
        for p in range(n_planes):
            plane_copy(p, k).wait_send()


def solution(mesh):
    nr, nc = mesh.shape["row"], mesh.shape["col"]

    def local(optical_field, index_panels):
        _, rows, cols = optical_field.shape
        n_planes, part, width = index_panels.shape
        wide = cols + LANES
        count = (rows + 2 * HALO) // part
        tall = rows + 2 * HALO + 2 * PAD
        grid = pltpu.VMEM((2, tall, wide), jnp.float32)
        return pl.pallas_call(
            functools.partial(kernel, nr, nc, 2),
            out_shape=jax.ShapeDtypeStruct(optical_field.shape, jnp.float32),
            in_specs=[pl.BlockSpec(memory_space=pltpu.HBM)] * 2,
            out_specs=pl.BlockSpec(memory_space=pltpu.VMEM),
            scratch_shapes=[
                pltpu.VMEM((n_planes, part, width), jnp.bfloat16),
                pltpu.VMEM((nc, part, LANES), jnp.bfloat16),
                pltpu.VMEM((count, part, LANES), jnp.bfloat16),
                pltpu.VMEM((n_planes, count, part, cols), jnp.bfloat16),
                pltpu.VMEM((n_planes - 1, count, part, LANES), jnp.bfloat16),
                grid, grid, grid, grid,
                pltpu.VMEM((2, 2, HALO, rows), jnp.float32),
                pltpu.VMEM((2, LANES, rows), jnp.float32),
                pltpu.VMEM((4, 2, HALO, LANES), jnp.float32),
                pltpu.SemaphoreType.DMA((3,)),
                pltpu.SemaphoreType.DMA((n_planes, nc)),
                pltpu.SemaphoreType.DMA((n_planes, nc)),
                pltpu.SemaphoreType.DMA((nc,)),
                pltpu.SemaphoreType.DMA((nc,)),
                pltpu.SemaphoreType.DMA((n_planes, 2)),
                pltpu.SemaphoreType.DMA((n_planes, 2)),
                pltpu.SemaphoreType.DMA((8,)),
                pltpu.SemaphoreType.DMA((8,)),
            ],
            compiler_params=pltpu.CompilerParams(
                collective_id=0, has_side_effects=True, vmem_limit_bytes=63 * 1024 * 1024),
        )(optical_field, index_panels)

    return jax.shard_map(
        local, mesh=mesh,
        in_specs=(P(None, "row", "col"), P(None, ("row", "col"), None)),
        out_specs=P(None, "row", "col"), check_vma=False,
    )
```

```python
import functools

import jax
import jax.numpy as jnp
from jax import lax
from jax.experimental import pallas as pl
from jax.experimental.pallas import tpu as pltpu
from jax.sharding import PartitionSpec as P

STEPS = 2
MESH = pl.DeviceIdType.MESH
HALO = 16
PAD = 8
LANES = 128

diffraction = 0.15
phase_gain = 0.25
near = diffraction * 16.0 / 12.0
far = diffraction / 12.0
mid = diffraction * 60.0 / 12.0


def kernel(nr, nc, ahead, field, panels_in, out, panels, pack, gathered, planes, edges, e, s1, s2, s3,
           strips, side, corners, load_sem, send_sem, plane_recv, edge_send, edge_recv, fwd_send, fwd_recv,
           halo_send, halo_recv):
    n_planes, part, width = panels.shape
    _, rows, cols = out.shape
    wide = cols + LANES
    sub = HALO // part
    blocks = rows // part
    top = PAD + HALO
    last = n_planes - 1
    pair = 2 * HALO
    r, c = lax.axis_index("row"), lax.axis_index("col")
    up, down = lax.rem(r + nr - 1, nr), lax.rem(r + 1, nr)
    left, right = lax.rem(c + nc - 1, nc), lax.rem(c + 1, nc)

    barrier = pltpu.get_barrier_semaphore()
    peers = [(r, lax.rem(c + k, nc)) for k in range(1, nc)]
    peers += [(y, x) for y in (up, down) for x in (left, c, right)]
    for peer in peers:
        pl.semaphore_signal(barrier, inc=1, device_id=peer, device_id_type=MESH)

    load_field = pltpu.make_async_copy(field, e.at[:, pl.ds(top, rows), pl.ds(0, cols)], load_sem.at[0])
    load_field.start()
    load_panels = pltpu.make_async_copy(panels_in, panels, load_sem.at[1])
    load_panels.start()
    own_columns = pl.ds(pl.multiple_of(c * cols, LANES), cols)
    own_planes = pltpu.make_async_copy(panels_in.at[:, :, own_columns], planes.at[:, sub + c], load_sem.at[2])
    own_planes.start()

    def plane_copy(p, k):
        to = lax.rem(c + k, nc)
        return pltpu.make_async_remote_copy(
            src_ref=panels_in.at[p, :, pl.ds(pl.multiple_of(to * cols, LANES), cols)],
            dst_ref=planes.at[p, sub + c],
            send_sem=send_sem.at[p, k], recv_sem=plane_recv.at[p, k],
            device_id=(r, to), device_id_type=MESH,
        )

    def send_plane(p):
        for k in range(1, nc):
            plane_copy(p, k).start()

    def edge_copy(k):
        to = lax.rem(c + k, nc)
        return pltpu.make_async_remote_copy(
            src_ref=pack.at[to], dst_ref=gathered.at[sub + c],
            send_sem=edge_send.at[k], recv_sem=edge_recv.at[k],
            device_id=(r, to), device_id_type=MESH,
        )

    def remote(src, dst, at, to):
        return pltpu.make_async_remote_copy(
            src_ref=src, dst_ref=dst, send_sem=halo_send.at[at], recv_sem=halo_recv.at[at],
            device_id=to, device_id_type=MESH,
        )

    low, high = pl.ds(0, HALO), pl.ds(rows - HALO, HALO)
    first_tile, last_tile = pl.ds(0, LANES), pl.ds(cols - LANES, LANES)
    halos = [
        remote(field.at[:, high, :], e.at[:, pl.ds(PAD, HALO), pl.ds(0, cols)], 0, (down, c)),
        remote(field.at[:, low, :], e.at[:, pl.ds(top + rows, HALO), pl.ds(0, cols)], 1, (up, c)),
        remote(strips.at[0], side.at[:, pl.ds(0, HALO), :], 2, (r, left)),
        remote(strips.at[1], side.at[:, pl.ds(LANES - HALO, HALO), :], 3, (r, right)),
        remote(field.at[:, high, first_tile], corners.at[0], 4, (down, left)),
        remote(field.at[:, high, last_tile], corners.at[1], 5, (down, right)),
        remote(field.at[:, low, first_tile], corners.at[2], 6, (up, left)),
        remote(field.at[:, low, last_tile], corners.at[3], 7, (up, right)),
    ]

    lane = lax.broadcasted_iota(jnp.int32, (part, LANES), 1)
    load_panels.wait()
    for d in range(nc):
        after = (d + 1) * cols % width
        before = (d * cols - LANES) % width
        tile = jnp.zeros((part, LANES), jnp.float32)
        for p in range(last):
            at = pair * p
            tile = jnp.where((lane >= at) & (lane < at + HALO), pltpu.roll(
                panels[p, :, after:after + LANES].astype(jnp.float32), at, 1), tile)
            at += HALO
            tile = jnp.where((lane >= at) & (lane < at + HALO), pltpu.roll(
                panels[p, :, before:before + LANES].astype(jnp.float32), (at + HALO) % LANES, 1), tile)
        pack[d] = tile.astype(pack.dtype)

    load_field.wait()
    for i in range(2):
        strips[0, i] = e[i, top:top + rows, 0:LANES].T[0:HALO]
        strips[1, i] = e[i, top:top + rows, cols - LANES:cols].T[LANES - HALO:LANES]

    pl.semaphore_wait(barrier, len(peers))
    for k in range(1, nc):
        edge_copy(k).start()
    for copy in halos:
        copy.start()
    for p in range(ahead):
        send_plane(p)
    gathered[sub + c] = pack[c]

    def forwards(ref, at):
        make = lambda src, dst, which, to: pltpu.make_async_remote_copy(
            src_ref=ref.at[pl.ds(src, sub)], dst_ref=ref.at[pl.ds(dst, sub)],
            send_sem=fwd_send.at[at, which], recv_sem=fwd_recv.at[at, which],
            device_id=(to, c), device_id_type=MESH,
        )
        return [make(blocks, 0, 0, down), make(sub, sub + blocks, 1, up)]

    for k in range(1, nc):
        edge_copy(k).wait_recv()
    edge_forwards = forwards(gathered, last)
    for copy in edge_forwards:
        copy.start()

    for copy in halos:
        copy.wait()
    tile_lane = lax.broadcasted_iota(jnp.int32, (HALO, LANES), 1)
    for i in range(2):
        e[i, top:top + rows, cols:wide] = side[i].T
        e[i, PAD:top, cols:wide] = jnp.where(tile_lane < LANES // 2, corners[0, i], corners[1, i])
        e[i, top + rows:top + rows + HALO, cols:wide] = jnp.where(
            tile_lane < LANES // 2, corners[2, i], corners[3, i])

    for copy in edge_forwards:
        copy.wait()
    for b in range(blocks + 2 * sub):
        tile = gathered[b].astype(jnp.float32)
        for p in range(last):
            edges[p, b] = jnp.where(
                lane < LANES // 2,
                pltpu.roll(tile, (LANES - pair * p) % LANES, 1),
                pltpu.roll(tile, (LANES - pair * (p + 1)) % LANES, 1),
            ).astype(edges.dtype)
    own_planes.wait()

    def take_plane(p):
        for k in range(1, nc):
            plane_copy(p, k).wait_recv()
        copies = forwards(planes.at[p], p) if p < last else []
        for copy in copies:
            copy.start()
        if p + ahead < n_planes:
            send_plane(p + ahead)
        return copies

    def evaluate(src, p, begin, end, finish, stride=1):
        def block(n, carry):
            b = n * stride
            row = pl.multiple_of(b * HALO, HALO)
            pieces = []
            for i in range(sub):
                piece = planes[p, b * sub + i].astype(jnp.float32)
                edge = edges[min(p, last - 1), b * sub + i].astype(jnp.float32)
                pieces.append(jnp.concatenate([piece, edge], axis=1))
            plane = pieces[0] if sub == 1 else jnp.concatenate(pieces, axis=0)
            factor = phase_gain * plane - mid
            totals = []
            for i in range(2):
                window = src[i, pl.ds(row, HALO + 2 * PAD), :]
                tall = HALO + 2 * PAD
                centre = window[PAD:PAD + HALO]
                shift_y = lambda n: pltpu.roll(window, n % tall, 0)[PAD:PAD + HALO]
                shift_x = lambda n: pltpu.roll(centre, n % wide, 1)
                one = (shift_y(1) + shift_y(-1)) + (shift_x(1) + shift_x(-1))
                two = (shift_y(2) + shift_y(-2)) + (shift_x(2) + shift_x(-2))
                totals.append(near * one - far * two + factor * centre)
            finish(pl.ds(pl.multiple_of(row + PAD, PAD), HALO), b, (-totals[1], totals[0]))
            return carry

        lax.fori_loop(begin, end, block, 0, unroll=end - begin)

    def stage(dst, weight):
        def finish(at, b, k):
            for i in range(2):
                dst[i, at, :] = e[i, at, :] + weight * k[i]
        return finish

    def close(at, b, k):
        for i in range(2):
            e[i, at, :] = (s1[i, at, :] + 2.0 * s2[i, at, :] + s3[i, at, :] - e[i, at, :]) * (1.0 / 3.0) + k[i] * (1.0 / 6.0)

    def close_out(at, b, k):
        here = pl.ds(pl.multiple_of((b - 1) * HALO, HALO), HALO)
        for i in range(2):
            value = (s1[i, at, :] + 2.0 * s2[i, at, :] + s3[i, at, :] - e[i, at, :]) * (1.0 / 3.0) + k[i] * (1.0 / 6.0)
            out[i, here, :] = value[:, 0:cols]

    full = rows // HALO + 2

    def first_evaluate(src, p, finish):
        copies = take_plane(p)
        evaluate(src, p, 1, full - 1, finish)
        for copy in copies:
            copy.wait()
        evaluate(src, p, 0, 2, finish, full - 1)

    for step in range(STEPS):
        p = 2 * step
        if step == 0:
            first_evaluate(e, p, stage(s1, 0.5))
        else:
            evaluate(e, p, 0, full, stage(s1, 0.5))
        first_evaluate(s1, p + 1, stage(s2, 0.5))
        evaluate(s2, p + 1, 0, full, stage(s3, 1.0))
        if step < STEPS - 1:
            first_evaluate(s3, p + 2, close)
        else:
            take_plane(p + 2)
            evaluate(s3, p + 2, 1, full - 1, close_out)

    for k in range(1, nc):
        edge_copy(k).wait_send()
        for p in range(n_planes):
            plane_copy(p, k).wait_send()


def solution(mesh):
    nr, nc = mesh.shape["row"], mesh.shape["col"]

    def local(optical_field, index_panels):
        _, rows, cols = optical_field.shape
        n_planes, part, width = index_panels.shape
        wide = cols + LANES
        count = (rows + 2 * HALO) // part
        tall = rows + 2 * HALO + 2 * PAD
        grid = pltpu.VMEM((2, tall, wide), jnp.float32)
        return pl.pallas_call(
            functools.partial(kernel, nr, nc, 2),
            out_shape=jax.ShapeDtypeStruct(optical_field.shape, jnp.float32),
            in_specs=[pl.BlockSpec(memory_space=pltpu.HBM)] * 2,
            out_specs=pl.BlockSpec(memory_space=pltpu.VMEM),
            scratch_shapes=[
                pltpu.VMEM((n_planes, part, width), jnp.bfloat16),
                pltpu.VMEM((nc, part, LANES), jnp.bfloat16),
                pltpu.VMEM((count, part, LANES), jnp.bfloat16),
                pltpu.VMEM((n_planes, count, part, cols), jnp.bfloat16),
                pltpu.VMEM((n_planes - 1, count, part, LANES), jnp.bfloat16),
                grid, grid, grid, grid,
                pltpu.VMEM((2, 2, HALO, rows), jnp.float32),
                pltpu.VMEM((2, LANES, rows), jnp.float32),
                pltpu.VMEM((4, 2, HALO, LANES), jnp.float32),
                pltpu.SemaphoreType.DMA((3,)),
                pltpu.SemaphoreType.DMA((n_planes, nc)),
                pltpu.SemaphoreType.DMA((n_planes, nc)),
                pltpu.SemaphoreType.DMA((nc,)),
                pltpu.SemaphoreType.DMA((nc,)),
                pltpu.SemaphoreType.DMA((n_planes, 2)),
                pltpu.SemaphoreType.DMA((n_planes, 2)),
                pltpu.SemaphoreType.DMA((8,)),
                pltpu.SemaphoreType.DMA((8,)),
            ],
            compiler_params=pltpu.CompilerParams(
                collective_id=0, has_side_effects=True, vmem_limit_bytes=63 * 1024 * 1024),
        )(optical_field, index_panels)

    return jax.shard_map(
        local, mesh=mesh,
        in_specs=(P(None, "row", "col"), P(None, ("row", "col"), None)),
        out_specs=P(None, "row", "col"), check_vma=False,
    )
```
